32 devices in a mesh: range: 16 (over z, y, x), chip: 2 (over core).
Axes of the slice: x: 2, y: 2, z: 4, core: 2. Of those that a mesh axis runs over, the one named last changes fastest.
Arguments:
- mode_tables: bfloat16 [32, 2048, 768], P('range', None, 'chip'), may hold values from -1 to 1
- attenuation: float32 [32, 768], P('range'), may hold values from 0 to 1, as said below
- excitation: float32 [768, 128], replicated, may hold values from -6 to 6
Outputs:
- fields: float32 [32, 2048, 128], P('range', 'chip')
The draws below stay inside these ranges and needn't reach their ends.
Inputs may be any that keep to these rules, and one draw needn't show every extreme that they name: attenuation rates, positive.
All inputs are finite; a program needn't handle non-finite values.
Results may differ from the reference program's by a relative error of at most 0.0029.
Values may be sent and summed in bfloat16 or wider, within the bound.
A program may use at most 64 MiB of HBM per device.

```python
import math
import jax
import jax.numpy as jnp
from jax import lax

MODES = 768
HEIGHTS = 2048
SOURCES = 128
RANGE_SEGMENTS = 32


def draw_mode_tables(key, part):
    base_key, noise_key = jax.random.split(jax.random.fold_in(key, 11))
    starting_value = jax.random.normal(base_key, (HEIGHTS, MODES), jnp.float32)
    ortho, _ = jnp.linalg.qr(starting_value)
    noise = jax.random.normal(noise_key, (RANGE_SEGMENTS, HEIGHTS, MODES), jnp.float32) * (0.082 / math.sqrt(HEIGHTS))
    return (ortho[None] + noise).astype(jnp.bfloat16)


def draw_attenuation(key, part):
    first_key, second_key, tertiary_key = jax.random.split(jax.random.fold_in(key, 23), 3)
    lowest = 0.3 / RANGE_SEGMENTS
    highest_rate = 0.03
    starting_value = jnp.exp(jax.random.uniform(first_key, (MODES,), jnp.float32, math.log(lowest), math.log(max(highest_rate, 2.0 * lowest))))
    multiplier = jnp.exp(jax.random.uniform(second_key, (RANGE_SEGMENTS, MODES), jnp.float32, math.log(0.5), math.log(2.0)))
    spike_positions = jax.random.randint(tertiary_key, (3,), 0, RANGE_SEGMENTS)
    spike_count = jnp.sum((jnp.arange(RANGE_SEGMENTS)[:, None] == spike_positions[None, :]).astype(jnp.float32), axis=1)
    return starting_value[None, :] * multiplier + 0.3 * spike_count[:, None]


def gaussian(key, extent, width, reach, held_as=jnp.bfloat16):
    return jnp.clip(width * jax.random.normal(key, extent, jnp.float32), -reach, reach).astype(held_as)


def setup_inputs(seed: int = 0) -> dict:
    splits = jax.random.split(jax.random.key(seed), 4)
    mode_tables = draw_mode_tables(jax.random.fold_in(splits[3], 71), 0)
    attenuation = draw_attenuation(jax.random.fold_in(splits[3], 71), 0)
    excitation = gaussian(splits[2], (MODES, SOURCES), 1.0, 6.0, jnp.float32)
    return dict(mode_tables=mode_tables, attenuation=attenuation, excitation=excitation)


highest = lax.Precision.HIGHEST

def widen(table):
    return table.astype(jnp.float32)

def field_of(table, amplitude):
    rounded = lax.optimization_barrier(amplitude.astype(jnp.bfloat16))
    return jnp.dot(widen(table), rounded.astype(jnp.float32), precision=highest)

def reference(mode_tables, attenuation, excitation):
    first_amplitude = jnp.exp(-attenuation[0])[:, None] * excitation

    def advance(state, inputs):
        amplitude, earlier = state
        current, damping_rates = inputs
        intersection = jnp.dot(widen(current).T, widen(earlier), precision=highest)
        matrix = jnp.exp(-damping_rates)[:, None] * intersection
        amplitude = jnp.dot(matrix, amplitude, precision=highest)
        return ((amplitude, current), field_of(current, amplitude))
    initial = (first_amplitude, mode_tables[0])
    _, later_fields = lax.scan(advance, initial, (mode_tables[1:], attenuation[1:]))
    first_field = field_of(mode_tables[0], first_amplitude)
    return jnp.concatenate([first_field[None], later_fields], axis=0)
```

```python
import functools

import jax
import jax.numpy as jnp
from jax import lax
from jax.experimental import pallas as pl
from jax.experimental.pallas import tpu as pltpu
from jax.sharding import PartitionSpec as P

MESH = pl.DeviceIdType.MESH
BF16, F32 = jnp.bfloat16, jnp.float32


def contract(a, b, da, db):
    return lax.dot_general(a, b, (((da,), (db,)), ((), ())), preferred_element_type=F32)


def split(x):
    hi = x.astype(BF16)
    return hi, (x - hi.astype(F32)).astype(BF16)


def times(x, w_hi, w_lo):
    rows = x.shape[0]
    hi, lo = split(x)
    both = contract(jnp.concatenate([hi, lo], axis=0), w_hi[...], 1, 0)
    return both[:rows] + (both[rows:] + contract(hi, w_lo[...], 1, 0))


def kernel(
    n, pieces, chunks,
    tab, att, exc, out,
    T, E, acc, m1, m0, pr, arrive, leave, rounded,
    load_sem, gat_s, gat_r, ear_s, ear_r, mat_s, mat_r, ch_s, ch_r, rd_s, rd_r,
):
    pos, core = lax.axis_index("range"), lax.axis_index("chip")
    other = 1 - core
    segs, heights, half = tab.shape
    modes = 2 * half
    own_cols = pl.ds(pl.multiple_of(core * half, 128), half)
    own_rows = pl.ds(pl.multiple_of(core * half, 128), half)
    partner, ahead, behind = (pos, other), (pos + 1, core), (pos - 1, core)
    has_next, has_prev = pos < n - 1, pos > 0

    loads = [
        pltpu.make_async_copy(tab.at[s], T.at[s, :, own_cols], load_sem.at[s]) for s in range(segs)
    ]
    for c in loads:
        c.start()
    barrier = pltpu.get_barrier_semaphore()
    pl.semaphore_signal(barrier, inc=1, device_id=partner, device_id_type=MESH)

    @pl.when(has_next)
    def _():
        pl.semaphore_signal(barrier, inc=1, device_id=ahead, device_id_type=MESH)

    @pl.when(has_prev)
    def _():
        pl.semaphore_signal(barrier, inc=1, device_id=behind, device_id_type=MESH)

    pl.semaphore_wait(barrier, 1 + has_next.astype(jnp.int32) + has_prev.astype(jnp.int32))

    def remote(src, dst, s, r, to):
        return pltpu.make_async_remote_copy(
            src_ref=src, dst_ref=dst, send_sem=s, recv_sem=r, device_id=to, device_id_type=MESH
        )

    gathers = [
        remote(tab.at[s], T.at[s, :, own_cols], gat_s.at[s], gat_r.at[s], partner)
        for s in range(segs)
    ]
    for c in gathers:
        c.start()
    size = heights // pieces

    def piece(i):
        rows = pl.ds(pl.multiple_of(i * size, 128), size)
        return remote(tab.at[segs - 1, rows], E.at[rows], ear_s.at[i], ear_r.at[i], ahead), rows

    @pl.when(has_next)
    def _():
        @pl.loop(0, pieces)
        def _(i):
            piece(i)[0].start()

    damp0, damp1 = jnp.exp(-att[0:1, :]), jnp.exp(-att[1:2, :])
    for c in loads:
        c.wait()
    for c in gathers:
        c.wait()

    @pl.loop(0, 2)
    def _(j):
        rows = pl.ds(pl.multiple_of(j * half, 128), half)
        m1[0, rows], m1[1, rows] = split(contract(T[0, :, rows], T[1], 0, 0) * damp1)

    @pl.when(jnp.logical_not(has_prev))
    def _():
        r = lax.broadcasted_iota(jnp.int32, (half, modes), 0) + core * half
        c = lax.broadcasted_iota(jnp.int32, (half, modes), 1)
        acc[...] = jnp.where(r == c, 1.0, 0.0).astype(F32)
        columns = exc[...].T
        count = chunks * arrive.shape[1]
        for k in range(2):
            @pl.when(core == k)
            def _():
                mine = columns[k * count:(k + 1) * count]
                arrive[...] = mine.reshape(arrive.shape)

    @pl.when(has_prev)
    def _():
        acc[...] = jnp.zeros_like(acc)

        @pl.loop(0, pieces)
        def _(i):
            copy, rows = piece(i)
            copy.wait_recv()
            acc[...] += contract(E[rows], T[0, rows], 0, 0)

    scaled = acc[...] * damp0
    m0[0, own_rows], m0[1, own_rows] = split(scaled)
    product = times(scaled, m1.at[0], m1.at[1])
    pr[0, own_rows], pr[1, own_rows] = split(product)
    mats = [
        remote(ref.at[k, own_rows], ref.at[k, own_rows], mat_s.at[2 * i + k], mat_r.at[2 * i + k], partner)
        for i, ref in enumerate((pr, m0)) for k in range(2)
    ]
    for c in mats:
        c.start()
    for c in mats[:2]:
        c.wait()

    def hop(k):
        return remote(leave.at[k], arrive.at[k], ch_s.at[k], ch_r.at[k], ahead)

    @pl.loop(0, chunks)
    def _(k):
        @pl.when(has_prev)
        def _():
            hop(k).wait_recv()

        leave[k] = times(arrive[k], pr.at[0], pr.at[1])

        @pl.when(has_next)
        def _():
            hop(k).start()

    for c in mats[2:]:
        c.wait()
    count = chunks * arrive.shape[1]
    mine = pl.ds(pl.multiple_of(core * count, 16), count)
    rounded[1, mine] = leave[...].reshape(count, modes).astype(BF16)
    late = remote(rounded.at[1, mine], rounded.at[1, mine], rd_s.at[1], rd_r.at[1], partner)
    late.start()
    rounded[0, mine] = times(arrive[...].reshape(count, modes), m0.at[0], m0.at[1]).astype(BF16)
    early = remote(rounded.at[0, mine], rounded.at[0, mine], rd_s.at[0], rd_r.at[0], partner)
    early.start()
    rows = heights // 2
    first = pl.multiple_of(core * rows, 128)
    for s, copy in ((1, late), (0, early)):
        copy.wait()
        out[s] = contract(T[s, pl.ds(first, rows)], rounded[s], 1, 1)

    @pl.when(has_next)
    def _():
        @pl.loop(0, pieces)
        def _(i):
            piece(i)[0].wait_send()

        @pl.loop(0, chunks)
        def _(k):
            hop(k).wait_send()


def solution(mesh):
    n, cores = mesh.shape["range"], mesh.shape["chip"]

    def on_device(tab, att, exc):
        segs, heights, half = tab.shape
        modes, sources = exc.shape
        pieces, chunks = 8, 4
        rows = sources // cores // chunks
        dma = pltpu.SemaphoreType.DMA
        vmem = pl.BlockSpec(memory_space=pltpu.VMEM)
        return pl.pallas_call(
            functools.partial(kernel, n, pieces, chunks),
            out_shape=jax.ShapeDtypeStruct((segs, heights // cores, sources), F32),
            in_specs=[pl.BlockSpec(memory_space=pl.ANY), vmem, vmem],
            out_specs=vmem,
            scratch_shapes=[
                pltpu.VMEM((segs, heights, modes), BF16),
                pltpu.VMEM((heights, half), BF16),
                pltpu.VMEM((half, modes), F32),
                pltpu.VMEM((2, modes, modes), BF16),
                pltpu.VMEM((2, modes, modes), BF16),
                pltpu.VMEM((2, modes, modes), BF16),
                pltpu.VMEM((chunks, rows, modes), F32),
                pltpu.VMEM((chunks, rows, modes), F32),
                pltpu.VMEM((segs, sources, modes), BF16),
                dma((segs,)),
                dma((segs,)), dma((segs,)),
                dma((pieces,)), dma((pieces,)),
                dma((4,)), dma((4,)),
                dma((chunks,)), dma((chunks,)),
                dma((2,)), dma((2,)),
            ],
            compiler_params=pltpu.CompilerParams(
                collective_id=0, has_side_effects=True, vmem_limit_bytes=60 * 2**20
            ),
        )(tab, att, exc)

    return jax.shard_map(
        on_device, mesh=mesh,
        in_specs=(P("range", None, "chip"), P("range", None), P()),
        out_specs=P("range", "chip", None), check_vma=False,
    )
```

```python
import functools

import jax
import jax.numpy as jnp
from jax import lax
from jax.experimental import pallas as pl
from jax.experimental.pallas import tpu as pltpu
from jax.sharding import PartitionSpec as P

MESH = pl.DeviceIdType.MESH
BF16, F32 = jnp.bfloat16, jnp.float32


def contract(a, b, da, db):
    return lax.dot_general(a, b, (((da,), (db,)), ((), ())), preferred_element_type=F32)


def split(x):
    hi = x.astype(BF16)
    return hi, (x - hi.astype(F32)).astype(BF16)


def stacked(x):
    hi = x.astype(BF16).astype(F32)
    return jnp.concatenate([hi, x - hi], axis=0).astype(BF16)


def times(x, w_hi, w_lo):
    rows = x.shape[0]
    both = contract(stacked(x), w_hi[...], 1, 0)
    return both[:rows] + (both[rows:] + contract(x.astype(BF16), w_lo[...], 1, 0))


def times_table(x, table, dim):
    rows = x.shape[0]
    both = contract(stacked(x), table, 1, dim)
    return both[:rows] + both[rows:]


def kernel(
    n, wide, pieces, chunks,
    tab, att, exc, out,
    T, E, acc, m1, m0, pr, arrive, leave, arrive_u, leave_u, early_a, rounded,
    load_sem, gat_s, gat_r, ear_s, ear_r, mat_s, mat_r, ch_s, ch_r, rd_s, rd_r,
):
    pos, core = lax.axis_index("range"), lax.axis_index("chip")
    other = 1 - core
    segs, heights, half = tab.shape
    modes = 2 * half
    own_cols = pl.ds(pl.multiple_of(core * half, 128), half)
    own_rows = pl.ds(pl.multiple_of(core * half, 128), half)
    partner, ahead, behind = (pos, other), (pos + 1, core), (pos - 1, core)
    has_next, has_prev = pos < n - 1, pos > 0
    wide_out, narrow_out = pos < wide, jnp.logical_and(pos >= wide, has_next)
    wide_in, narrow_in = jnp.logical_and(has_prev, pos <= wide), pos > wide

    loads = [
        pltpu.make_async_copy(tab.at[s], T.at[s, :, own_cols], load_sem.at[s]) for s in range(segs)
    ]
    for c in loads:
        c.start()
    barrier = pltpu.get_barrier_semaphore()
    pl.semaphore_signal(barrier, inc=1, device_id=partner, device_id_type=MESH)

    @pl.when(has_next)
    def _():
        pl.semaphore_signal(barrier, inc=1, device_id=ahead, device_id_type=MESH)

    @pl.when(has_prev)
    def _():
        pl.semaphore_signal(barrier, inc=1, device_id=behind, device_id_type=MESH)

    pl.semaphore_wait(barrier, 1 + has_next.astype(jnp.int32) + has_prev.astype(jnp.int32))

    def remote(src, dst, s, r, to):
        return pltpu.make_async_remote_copy(
            src_ref=src, dst_ref=dst, send_sem=s, recv_sem=r, device_id=to, device_id_type=MESH
        )

    gathers = [
        remote(tab.at[s], T.at[s, :, own_cols], gat_s.at[s], gat_r.at[s], partner)
        for s in range(segs)
    ]
    for c in gathers:
        c.start()
    size = heights // pieces

    def piece(i):
        rows = pl.ds(pl.multiple_of(i * size, 128), size)
        return remote(tab.at[segs - 1, rows], E.at[rows], ear_s.at[i], ear_r.at[i], ahead), rows

    @pl.when(narrow_out)
    def _():
        @pl.loop(0, pieces)
        def _(i):
            piece(i)[0].start()

    damp0, damp1 = jnp.exp(-att[0:1, :]), jnp.exp(-att[1:2, :])
    for c in loads:
        c.wait()
    for c in gathers:
        c.wait()

    @pl.loop(0, 2)
    def _(j):
        rows = pl.ds(pl.multiple_of(j * half, 128), half)
        m1[0, rows], m1[1, rows] = split(contract(T[0, :, rows], T[1], 0, 0) * damp1)

    count = chunks * arrive.shape[1]

    def hop(k):
        return remote(leave.at[k], arrive.at[k], ch_s.at[k], ch_r.at[k], ahead)

    def wide_hop(k):
        return remote(leave_u.at[k], arrive_u.at[k], ch_s.at[k], ch_r.at[k], ahead)

    def send(k):
        @pl.when(wide_out)
        def _():
            leave_u[k] = times_table(leave[k], T[1], 1)
            wide_hop(k).start()

        @pl.when(narrow_out)
        def _():
            hop(k).start()

    @pl.when(jnp.logical_not(has_prev))
    def _():
        columns = exc[...].T
        for k in range(2):
            @pl.when(core == k)
            def _():
                start = columns[k * count:(k + 1) * count] * damp0
                early_a[...] = start.reshape(early_a.shape)

        start = early_a[...].reshape(count, modes)
        leave[...] = times(start, m1.at[0], m1.at[1]).reshape(leave.shape)

        @pl.loop(0, chunks)
        def _(k):
            send(k)

    @pl.when(wide_in)
    def _():
        @pl.loop(0, chunks)
        def _(k):
            wide_hop(k).wait_recv()
            value = times_table(arrive_u[k], T[0], 0) * damp0
            early_a[k] = value
            leave[k] = times(value, m1.at[0], m1.at[1])
            send(k)

    @pl.when(narrow_in)
    def _():
        acc[...] = jnp.zeros_like(acc)

        @pl.loop(0, pieces)
        def _(i):
            copy, rows = piece(i)
            copy.wait_recv()
            acc[...] += contract(E[rows], T[0, rows], 0, 0)

        scaled = acc[...] * damp0
        m0[0, own_rows], m0[1, own_rows] = split(scaled)
        product = times(scaled, m1.at[0], m1.at[1])
        pr[0, own_rows], pr[1, own_rows] = split(product)
        mats = [
            remote(ref.at[k, own_rows], ref.at[k, own_rows], mat_s.at[2 * i + k], mat_r.at[2 * i + k], partner)
            for i, ref in enumerate((pr, m0)) for k in range(2)
        ]
        for c in mats:
            c.start()
        for c in mats[:2]:
            c.wait()

        @pl.loop(0, chunks)
        def _(k):
            hop(k).wait_recv()
            leave[k] = times(arrive[k], pr.at[0], pr.at[1])
            send(k)

        for c in mats[2:]:
            c.wait()
        value = times(arrive[...].reshape(count, modes), m0.at[0], m0.at[1])
        early_a[...] = value.reshape(early_a.shape)

    mine = pl.ds(pl.multiple_of(core * count, 16), count)
    rounded[1, mine] = leave[...].reshape(count, modes).astype(BF16)
    late = remote(rounded.at[1, mine], rounded.at[1, mine], rd_s.at[1], rd_r.at[1], partner)
    late.start()
    rounded[0, mine] = early_a[...].reshape(count, modes).astype(BF16)
    early = remote(rounded.at[0, mine], rounded.at[0, mine], rd_s.at[0], rd_r.at[0], partner)
    early.start()
    rows = heights // 2
    first = pl.multiple_of(core * rows, 128)
    for s, copy in ((1, late), (0, early)):
        copy.wait()
        out[s] = contract(T[s, pl.ds(first, rows)], rounded[s], 1, 1)

    @pl.when(narrow_out)
    def _():
        @pl.loop(0, pieces)
        def _(i):
            piece(i)[0].wait_send()

        @pl.loop(0, chunks)
        def _(k):
            hop(k).wait_send()

    @pl.when(wide_out)
    def _():
        @pl.loop(0, chunks)
        def _(k):
            wide_hop(k).wait_send()


def solution(mesh):
    n, cores = mesh.shape["range"], mesh.shape["chip"]

    def on_device(tab, att, exc):
        segs, heights, half = tab.shape
        modes, sources = exc.shape
        wide, pieces, chunks = min(4, n - 1), 8, 8
        rows = sources // cores // chunks
        dma = pltpu.SemaphoreType.DMA
        vmem = pl.BlockSpec(memory_space=pltpu.VMEM)
        return pl.pallas_call(
            functools.partial(kernel, n, wide, pieces, chunks),
            out_shape=jax.ShapeDtypeStruct((segs, heights // cores, sources), F32),
            in_specs=[pl.BlockSpec(memory_space=pl.ANY), vmem, vmem],
            out_specs=vmem,
            scratch_shapes=[
                pltpu.VMEM((segs, heights, modes), BF16),
                pltpu.VMEM((heights, half), BF16),
                pltpu.VMEM((half, modes), F32),
                pltpu.VMEM((2, modes, modes), BF16),
                pltpu.VMEM((2, modes, modes), BF16),
                pltpu.VMEM((2, modes, modes), BF16),
                pltpu.VMEM((chunks, rows, modes), F32),
                pltpu.VMEM((chunks, rows, modes), F32),
                pltpu.VMEM((chunks, rows, heights), F32),
                pltpu.VMEM((chunks, rows, heights), F32),
                pltpu.VMEM((chunks, rows, modes), F32),
                pltpu.VMEM((segs, sources, modes), BF16),
                dma((segs,)),
                dma((segs,)), dma((segs,)),
                dma((pieces,)), dma((pieces,)),
                dma((4,)), dma((4,)),
                dma((chunks,)), dma((chunks,)),
                dma((2,)), dma((2,)),
            ],
            compiler_params=pltpu.CompilerParams(
                collective_id=0, has_side_effects=True, vmem_limit_bytes=60 * 2**20
            ),
        )(tab, att, exc)

    return jax.shard_map(
        on_device, mesh=mesh,
        in_specs=(P("range", None, "chip"), P("range", None), P()),
        out_specs=P("range", "chip", None), check_vma=False,
    )
```

```python
import functools

import jax
import jax.numpy as jnp
from jax import lax
from jax.experimental import pallas as pl
from jax.experimental.pallas import tpu as pltpu
from jax.sharding import PartitionSpec as P

MESH = pl.DeviceIdType.MESH
BF16, F32 = jnp.bfloat16, jnp.float32


def contract(a, b, da, db):
    return lax.dot_general(a, b, (((da,), (db,)), ((), ())), preferred_element_type=F32)


def split(x):
    hi = x.astype(BF16)
    return hi, (x - hi.astype(F32)).astype(BF16)


def stacked(x):
    hi = x.astype(BF16).astype(F32)
    return jnp.concatenate([hi, x - hi], axis=0).astype(BF16)


def times(x, w_hi, w_lo):
    rows = x.shape[0]
    both = contract(stacked(x), w_hi[...], 1, 0)
    return both[:rows] + (both[rows:] + contract(x.astype(BF16), w_lo[...], 1, 0))


def times_table(x, table, dim):
    rows = x.shape[0]
    both = contract(stacked(x), table, 1, dim)
    return both[:rows] + both[rows:]


def kernel(
    n, wide, pieces, chunks,
    tab, att, exc, out,
    T, E, acc, m1, m0, pr, arrive, leave, arrive_u, leave_u, early_a, late_r, rounded,
    load_sem, gat_s, gat_r, ear_s, ear_r, mat_s, mat_r, ch_s, ch_r, rd_s, rd_r,
):
    pos, core = lax.axis_index("range"), lax.axis_index("chip")
    other = 1 - core
    segs, heights, half = tab.shape
    modes = 2 * half
    own_cols = pl.ds(pl.multiple_of(core * half, 128), half)
    own_rows = pl.ds(pl.multiple_of(core * half, 128), half)
    partner, ahead, behind = (pos, other), (pos + 1, core), (pos - 1, core)
    has_next, has_prev = pos < n - 1, pos > 0
    wide_out, narrow_out = pos < wide, jnp.logical_and(pos >= wide, has_next)
    wide_in, narrow_in = jnp.logical_and(has_prev, pos <= wide), pos > wide

    loads = [
        pltpu.make_async_copy(tab.at[s], T.at[s, :, own_cols], load_sem.at[s]) for s in range(segs)
    ]
    for c in loads:
        c.start()
    barrier = pltpu.get_barrier_semaphore()
    pl.semaphore_signal(barrier, inc=1, device_id=partner, device_id_type=MESH)

    @pl.when(has_next)
    def _():
        pl.semaphore_signal(barrier, inc=1, device_id=ahead, device_id_type=MESH)

    @pl.when(has_prev)
    def _():
        pl.semaphore_signal(barrier, inc=1, device_id=behind, device_id_type=MESH)

    pl.semaphore_wait(barrier, 1 + has_next.astype(jnp.int32) + has_prev.astype(jnp.int32))

    def remote(src, dst, s, r, to):
        return pltpu.make_async_remote_copy(
            src_ref=src, dst_ref=dst, send_sem=s, recv_sem=r, device_id=to, device_id_type=MESH
        )

    gathers = [
        remote(tab.at[s], T.at[s, :, own_cols], gat_s.at[s], gat_r.at[s], partner)
        for s in range(segs)
    ]
    for c in gathers:
        c.start()
    size = heights // pieces

    def piece(i):
        rows = pl.ds(pl.multiple_of(i * size, 128), size)
        return remote(tab.at[segs - 1, rows], E.at[rows], ear_s.at[i], ear_r.at[i], ahead), rows

    @pl.when(narrow_out)
    def _():
        @pl.loop(0, pieces)
        def _(i):
            piece(i)[0].start()

    damp0, damp1 = jnp.exp(-att[0:1, :]), jnp.exp(-att[1:2, :])
    for c in loads:
        c.wait()
    for c in gathers:
        c.wait()

    @pl.when(has_prev)
    def _():
        @pl.loop(0, 2)
        def _(j):
            rows = pl.ds(pl.multiple_of(j * half, 128), half)
            m1[0, rows], m1[1, rows] = split(contract(T[0, :, rows], T[1], 0, 0) * damp1)

    count = chunks * arrive.shape[1]

    def hop(k):
        return remote(leave.at[k], arrive.at[k], ch_s.at[k], ch_r.at[k], ahead)

    def wide_hop(k):
        return remote(leave_u.at[k], arrive_u.at[k], ch_s.at[k], ch_r.at[k], ahead)

    def late(k):
        mine = late_r.at[core, k]
        return remote(mine, mine, rd_s.at[k], rd_r.at[k], partner)

    def send(k):
        @pl.when(wide_out)
        def _():
            leave_u[k] = times_table(leave[k], T[1], 1)
            wide_hop(k).start()

        @pl.when(narrow_out)
        def _():
            hop(k).start()

        late_r[core, k] = leave[k].astype(BF16)
        late(k).start()

    @pl.when(jnp.logical_not(has_prev))
    def _():
        columns = exc[...].T
        for k in range(2):
            @pl.when(core == k)
            def _():
                start = columns[k * count:(k + 1) * count] * damp0
                early_a[...] = start.reshape(early_a.shape)

        start = early_a[...].reshape(count, modes)
        value = times_table(times_table(start, T[0], 1), T[1], 0) * damp1
        leave[...] = value.reshape(leave.shape)

        @pl.loop(0, chunks)
        def _(k):
            send(k)

    @pl.when(wide_in)
    def _():
        @pl.loop(0, chunks)
        def _(k):
            wide_hop(k).wait_recv()
            value = times_table(arrive_u[k], T[0], 0) * damp0
            early_a[k] = value
            leave[k] = times(value, m1.at[0], m1.at[1])
            send(k)

    @pl.when(narrow_in)
    def _():
        acc[...] = jnp.zeros_like(acc)

        @pl.loop(0, pieces)
        def _(i):
            copy, rows = piece(i)
            copy.wait_recv()
            acc[...] += contract(E[rows], T[0, rows], 0, 0)

        scaled = acc[...] * damp0
        m0[0, own_rows], m0[1, own_rows] = split(scaled)
        product = times(scaled, m1.at[0], m1.at[1])
        pr[0, own_rows], pr[1, own_rows] = split(product)
        mats = [
            remote(ref.at[k, own_rows], ref.at[k, own_rows], mat_s.at[2 * i + k], mat_r.at[2 * i + k], partner)
            for i, ref in enumerate((pr, m0)) for k in range(2)
        ]
        for c in mats:
            c.start()
        for c in mats[:2]:
            c.wait()

        @pl.loop(0, chunks)
        def _(k):
            hop(k).wait_recv()
            leave[k] = times(arrive[k], pr.at[0], pr.at[1])
            send(k)

        for c in mats[2:]:
            c.wait()
        value = times(arrive[...].reshape(count, modes), m0.at[0], m0.at[1])
        early_a[...] = value.reshape(early_a.shape)

    mine = pl.ds(pl.multiple_of(core * count, 16), count)
    rounded[mine] = early_a[...].reshape(count, modes).astype(BF16)
    early = remote(rounded.at[mine], rounded.at[mine], rd_s.at[chunks], rd_r.at[chunks], partner)
    early.start()
    rows = heights // 2
    first = pl.multiple_of(core * rows, 128)

    @pl.loop(0, chunks)
    def _(k):
        late(k).wait()

    out[1] = contract(T[1, pl.ds(first, rows)], late_r[...].reshape(rounded.shape), 1, 1)
    early.wait()
    out[0] = contract(T[0, pl.ds(first, rows)], rounded[...], 1, 1)

    @pl.when(narrow_out)
    def _():
        @pl.loop(0, pieces)
        def _(i):
            piece(i)[0].wait_send()

        @pl.loop(0, chunks)
        def _(k):
            hop(k).wait_send()

    @pl.when(wide_out)
    def _():
        @pl.loop(0, chunks)
        def _(k):
            wide_hop(k).wait_send()


def solution(mesh):
    n, cores = mesh.shape["range"], mesh.shape["chip"]

    def on_device(tab, att, exc):
        segs, heights, half = tab.shape
        modes, sources = exc.shape
        wide, pieces, chunks = min(4, n - 1), 8, 8
        rows = sources // cores // chunks
        dma = pltpu.SemaphoreType.DMA
        vmem = pl.BlockSpec(memory_space=pltpu.VMEM)
        return pl.pallas_call(
            functools.partial(kernel, n, wide, pieces, chunks),
            out_shape=pltpu.VMEM((segs, heights // cores, sources), F32),
            in_specs=[pl.BlockSpec(memory_space=pl.ANY), vmem, vmem],
            out_specs=vmem,
            scratch_shapes=[
                pltpu.VMEM((segs, heights, modes), BF16),
                pltpu.VMEM((heights, half), BF16),
                pltpu.VMEM((half, modes), F32),
                pltpu.VMEM((2, modes, modes), BF16),
                pltpu.VMEM((2, modes, modes), BF16),
                pltpu.VMEM((2, modes, modes), BF16),
                pltpu.VMEM((chunks, rows, modes), F32),
                pltpu.VMEM((chunks, rows, modes), F32),
                pltpu.VMEM((chunks, rows, heights), F32),
                pltpu.VMEM((chunks, rows, heights), F32),
                pltpu.VMEM((chunks, rows, modes), F32),
                pltpu.VMEM((cores, chunks, rows, modes), BF16),
                pltpu.VMEM((sources, modes), BF16),
                dma((segs,)),
                dma((segs,)), dma((segs,)),
                dma((pieces,)), dma((pieces,)),
                dma((4,)), dma((4,)),
                dma((chunks,)), dma((chunks,)),
                dma((chunks + 1,)), dma((chunks + 1,)),
            ],
            compiler_params=pltpu.CompilerParams(
                collective_id=0, has_side_effects=True, vmem_limit_bytes=60 * 2**20
            ),
        )(tab, att, exc)

    return jax.shard_map(
        on_device, mesh=mesh,
        in_specs=(P("range", None, "chip"), P("range", None), P()),
        out_specs=P("range", "chip", None), check_vma=False,
    )
```

```python
import functools

import jax
import jax.numpy as jnp
from jax import lax
from jax.experimental import pallas as pl
from jax.experimental.pallas import tpu as pltpu
from jax.sharding import PartitionSpec as P

MESH = pl.DeviceIdType.MESH
BF16, F32 = jnp.bfloat16, jnp.float32


def contract(a, b, da, db):
    return lax.dot_general(a, b, (((da,), (db,)), ((), ())), preferred_element_type=F32)


def split(x):
    hi = x.astype(BF16)
    return hi, (x - hi.astype(F32)).astype(BF16)


def stacked(x):
    hi = x.astype(BF16).astype(F32)
    return jnp.concatenate([hi, x - hi], axis=0).astype(BF16)


def times(x, w_hi, w_lo):
    rows = x.shape[0]
    both = contract(stacked(x), w_hi[...], 1, 0)
    return both[:rows] + (both[rows:] + contract(x.astype(BF16), w_lo[...], 1, 0))


def times_table(x, table, dim):
    rows = x.shape[0]
    both = contract(stacked(x), table, 1, dim)
    return both[:rows] + both[rows:]


def kernel(
    n, wide, pieces, chunks,
    tab, att, exc, out,
    T, E, acc, m1, m0, pr, arrive, leave, arrive_u, leave_u, early_a, late_r, rounded,
    load_sem, gat_s, gat_r, ear_s, ear_r, mat_s, mat_r, ch_s, ch_r, wd_s, wd_r, rd_s, rd_r,
):
    pos, core = lax.axis_index("range"), lax.axis_index("chip")
    other = 1 - core
    segs, heights, half = tab.shape
    modes = 2 * half
    own_cols = pl.ds(pl.multiple_of(core * half, 128), half)
    own_rows = pl.ds(pl.multiple_of(core * half, 128), half)
    partner, ahead, behind = (pos, other), (pos + 1, core), (pos - 1, core)
    has_next, has_prev = pos < n - 1, pos > 0
    wide_out, narrow_out = pos < wide, jnp.logical_and(pos >= wide, has_next)
    wide_in, narrow_in = jnp.logical_and(has_prev, pos <= wide), pos > wide

    loads = [
        pltpu.make_async_copy(tab.at[s], T.at[s, :, own_cols], load_sem.at[s]) for s in range(segs)
    ]
    for c in loads:
        c.start()
    barrier = pltpu.get_barrier_semaphore()
    pl.semaphore_signal(barrier, inc=1, device_id=partner, device_id_type=MESH)

    @pl.when(has_next)
    def _():
        pl.semaphore_signal(barrier, inc=1, device_id=ahead, device_id_type=MESH)

    @pl.when(has_prev)
    def _():
        pl.semaphore_signal(barrier, inc=1, device_id=behind, device_id_type=MESH)

    pl.semaphore_wait(barrier, 1 + has_next.astype(jnp.int32) + has_prev.astype(jnp.int32))

    def remote(src, dst, s, r, to):
        return pltpu.make_async_remote_copy(
            src_ref=src, dst_ref=dst, send_sem=s, recv_sem=r, device_id=to, device_id_type=MESH
        )

    gathers = [
        remote(tab.at[s], T.at[s, :, own_cols], gat_s.at[s], gat_r.at[s], partner)
        for s in range(segs)
    ]
    for c in gathers:
        c.start()
    size = heights // pieces

    def piece(i):
        rows = pl.ds(pl.multiple_of(i * size, 128), size)
        return remote(tab.at[segs - 1, rows], E.at[rows], ear_s.at[i], ear_r.at[i], ahead), rows

    @pl.when(narrow_out)
    def _():
        @pl.loop(0, pieces)
        def _(i):
            piece(i)[0].start()

    damp0, damp1 = jnp.exp(-att[0:1, :]), jnp.exp(-att[1:2, :])
    for c in loads:
        c.wait()
    for c in gathers:
        c.wait()

    @pl.when(has_prev)
    def _():
        @pl.loop(0, 2)
        def _(j):
            rows = pl.ds(pl.multiple_of(j * half, 128), half)
            m1[0, rows], m1[1, rows] = split(contract(T[0, :, rows], T[1], 0, 0) * damp1)

    count = chunks * arrive.shape[1]

    def hop(k):
        return remote(leave.at[k], arrive.at[k], ch_s.at[k], ch_r.at[k], ahead)

    parts = leave_u.shape[0]
    depth = heights // parts

    def wide_hop(k, p):
        return remote(leave_u.at[p, k], arrive_u.at[p, k], wd_s.at[p, k], wd_r.at[p, k], ahead)

    def late(k):
        mine = late_r.at[core, k]
        return remote(mine, mine, rd_s.at[k], rd_r.at[k], partner)

    def send(k):
        @pl.when(wide_out)
        def _():
            for p in range(parts):
                leave_u[p, k] = times_table(leave[k], T[1, p * depth:(p + 1) * depth], 1)
                wide_hop(k, p).start()

        @pl.when(narrow_out)
        def _():
            hop(k).start()

        late_r[core, k] = leave[k].astype(BF16)
        late(k).start()

    @pl.when(jnp.logical_not(has_prev))
    def _():
        columns = exc[...].T
        for k in range(2):
            @pl.when(core == k)
            def _():
                start = columns[k * count:(k + 1) * count] * damp0
                early_a[...] = start.reshape(early_a.shape)

        start = early_a[...].reshape(count, modes)
        value = times_table(times_table(start, T[0], 1), T[1], 0) * damp1
        leave[...] = value.reshape(leave.shape)

        @pl.loop(0, chunks)
        def _(k):
            send(k)

    @pl.when(wide_in)
    def _():
        @pl.loop(0, chunks)
        def _(k):
            value = jnp.zeros(leave.shape[1:], F32)
            for p in range(parts):
                wide_hop(k, p).wait_recv()
                value += times_table(arrive_u[p, k], T[0, p * depth:(p + 1) * depth], 0)
            value = value * damp0
            early_a[k] = value
            leave[k] = times(value, m1.at[0], m1.at[1])
            send(k)

    @pl.when(narrow_in)
    def _():
        acc[...] = jnp.zeros_like(acc)

        @pl.loop(0, pieces)
        def _(i):
            copy, rows = piece(i)
            copy.wait_recv()
            acc[...] += contract(E[rows], T[0, rows], 0, 0)

        scaled = acc[...] * damp0
        m0[0, own_rows], m0[1, own_rows] = split(scaled)
        product = times(scaled, m1.at[0], m1.at[1])
        pr[0, own_rows], pr[1, own_rows] = split(product)
        mats = [
            remote(ref.at[k, own_rows], ref.at[k, own_rows], mat_s.at[2 * i + k], mat_r.at[2 * i + k], partner)
            for i, ref in enumerate((pr, m0)) for k in range(2)
        ]
        for c in mats:
            c.start()
        for c in mats[:2]:
            c.wait()

        @pl.loop(0, chunks)
        def _(k):
            hop(k).wait_recv()
            leave[k] = times(arrive[k], pr.at[0], pr.at[1])
            send(k)

        for c in mats[2:]:
            c.wait()
        value = times(arrive[...].reshape(count, modes), m0.at[0], m0.at[1])
        early_a[...] = value.reshape(early_a.shape)

    mine = pl.ds(pl.multiple_of(core * count, 16), count)
    rounded[mine] = early_a[...].reshape(count, modes).astype(BF16)
    early = remote(rounded.at[mine], rounded.at[mine], rd_s.at[chunks], rd_r.at[chunks], partner)
    early.start()
    rows = heights // 2
    first = pl.multiple_of(core * rows, 128)

    @pl.loop(0, chunks)
    def _(k):
        late(k).wait()

    out[1] = contract(T[1, pl.ds(first, rows)], late_r[...].reshape(rounded.shape), 1, 1)
    early.wait()
    out[0] = contract(T[0, pl.ds(first, rows)], rounded[...], 1, 1)

    @pl.when(narrow_out)
    def _():
        @pl.loop(0, pieces)
        def _(i):
            piece(i)[0].wait_send()

        @pl.loop(0, chunks)
        def _(k):
            hop(k).wait_send()

    @pl.when(wide_out)
    def _():
        @pl.loop(0, chunks)
        def _(k):
            for p in range(parts):
                wide_hop(k, p).wait_send()


def solution(mesh):
    n, cores = mesh.shape["range"], mesh.shape["chip"]

    def on_device(tab, att, exc):
        segs, heights, half = tab.shape
        modes, sources = exc.shape
        wide, pieces, chunks, parts = min(4, n - 1), 8, 8, 2
        rows = sources // cores // chunks
        dma = pltpu.SemaphoreType.DMA
        vmem = pl.BlockSpec(memory_space=pltpu.VMEM)
        return pl.pallas_call(
            functools.partial(kernel, n, wide, pieces, chunks),
            out_shape=pltpu.VMEM((segs, heights // cores, sources), F32),
            in_specs=[pl.BlockSpec(memory_space=pl.ANY), vmem, vmem],
            out_specs=vmem,
            scratch_shapes=[
                pltpu.VMEM((segs, heights, modes), BF16),
                pltpu.VMEM((heights, half), BF16),
                pltpu.VMEM((half, modes), F32),
                pltpu.VMEM((2, modes, modes), BF16),
                pltpu.VMEM((2, modes, modes), BF16),
                pltpu.VMEM((2, modes, modes), BF16),
                pltpu.VMEM((chunks, rows, modes), F32),
                pltpu.VMEM((chunks, rows, modes), F32),
                pltpu.VMEM((parts, chunks, rows, heights // parts), F32),
                pltpu.VMEM((parts, chunks, rows, heights // parts), F32),
                pltpu.VMEM((chunks, rows, modes), F32),
                pltpu.VMEM((cores, chunks, rows, modes), BF16),
                pltpu.VMEM((sources, modes), BF16),
                dma((segs,)),
                dma((segs,)), dma((segs,)),
                dma((pieces,)), dma((pieces,)),
                dma((4,)), dma((4,)),
                dma((chunks,)), dma((chunks,)),
                dma((parts, chunks)), dma((parts, chunks)),
                dma((chunks + 1,)), dma((chunks + 1,)),
            ],
            compiler_params=pltpu.CompilerParams(
                collective_id=0, has_side_effects=True, vmem_limit_bytes=60 * 2**20
            ),
        )(tab, att, exc)

    return jax.shard_map(
        on_device, mesh=mesh,
        in_specs=(P("range", None, "chip"), P("range", None), P()),
        out_specs=P("range", "chip", None), check_vma=False,
    )
```

```python
import functools

import jax
import jax.numpy as jnp
from jax import lax
from jax.experimental import pallas as pl
from jax.experimental.pallas import tpu as pltpu
from jax.sharding import PartitionSpec as P

MESH = pl.DeviceIdType.MESH
BF16, F32 = jnp.bfloat16, jnp.float32


def contract(a, b, da, db):
    return lax.dot_general(a, b, (((da,), (db,)), ((), ())), preferred_element_type=F32)


def split(x):
    hi = x.astype(BF16)
    return hi, (x - hi.astype(F32)).astype(BF16)


def stacked(x):
    hi = x.astype(BF16).astype(F32)
    return jnp.concatenate([hi, x - hi], axis=0).astype(BF16)


def times(x, w_hi, w_lo):
    rows = x.shape[0]
    both = contract(stacked(x), w_hi[...], 1, 0)
    return both[:rows] + (both[rows:] + contract(x.astype(BF16), w_lo[...], 1, 0))


def times_table(x, table, dim):
    rows = x.shape[0]
    both = contract(stacked(x), table, 1, dim)
    return both[:rows] + both[rows:]


def kernel(
    n, wide, pieces, chunks,
    tab, att, exc, out,
    T, E, acc, m1, m0, pr, arrive, leave, arrive_u, leave_u, early_a, late_r, rounded,
    load_sem, gat_s, gat_r, ear_s, ear_r, mat_s, mat_r, ch_s, ch_r, wd_s, wd_r, rd_s, rd_r,
):
    pos, core = lax.axis_index("range"), lax.axis_index("chip")
    other = 1 - core
    segs, heights, half = tab.shape
    modes = 2 * half
    own_cols = pl.ds(pl.multiple_of(core * half, 128), half)
    own_rows = pl.ds(pl.multiple_of(core * half, 128), half)
    partner, ahead, behind = (pos, other), (pos + 1, core), (pos - 1, core)
    has_next, has_prev = pos < n - 1, pos > 0
    wide_out, narrow_out = pos < wide, jnp.logical_and(pos >= wide, has_next)
    wide_in, narrow_in = jnp.logical_and(has_prev, pos <= wide), pos > wide

    loads = [
        pltpu.make_async_copy(tab.at[s], T.at[s, :, own_cols], load_sem.at[s]) for s in range(segs)
    ]
    for c in loads:
        c.start()
    barrier = pltpu.get_barrier_semaphore()
    pl.semaphore_signal(barrier, inc=1, device_id=partner, device_id_type=MESH)

    @pl.when(has_next)
    def _():
        pl.semaphore_signal(barrier, inc=1, device_id=ahead, device_id_type=MESH)

    @pl.when(has_prev)
    def _():
        pl.semaphore_signal(barrier, inc=1, device_id=behind, device_id_type=MESH)

    pl.semaphore_wait(barrier, 1 + has_next.astype(jnp.int32) + has_prev.astype(jnp.int32))

    def remote(src, dst, s, r, to):
        return pltpu.make_async_remote_copy(
            src_ref=src, dst_ref=dst, send_sem=s, recv_sem=r, device_id=to, device_id_type=MESH
        )

    gathers = [
        remote(tab.at[s], T.at[s, :, own_cols], gat_s.at[s], gat_r.at[s], partner)
        for s in range(segs)
    ]
    for c in gathers:
        c.start()
    size = heights // pieces

    def piece(i):
        rows = pl.ds(pl.multiple_of(i * size, 128), size)
        return remote(tab.at[segs - 1, rows], E.at[rows], ear_s.at[i], ear_r.at[i], ahead), rows

    @pl.when(narrow_out)
    def _():
        @pl.loop(0, pieces)
        def _(i):
            piece(i)[0].start()

    damp0, damp1 = jnp.exp(-att[0:1, :]), jnp.exp(-att[1:2, :])
    for c in loads:
        c.wait()
    for c in gathers:
        c.wait()

    @pl.when(has_prev)
    def _():
        @pl.loop(0, 2)
        def _(j):
            rows = pl.ds(pl.multiple_of(j * half, 128), half)
            m1[0, rows], m1[1, rows] = split(contract(T[0, :, rows], T[1], 0, 0) * damp1)

    count = chunks * arrive.shape[1]

    def hop(k):
        return remote(leave.at[k], arrive.at[k], ch_s.at[k], ch_r.at[k], ahead)

    parts = leave_u.shape[0]
    depth = heights // parts
    wides = leave_u.shape[1]
    group = chunks // wides

    def wide_hop(k, p):
        return remote(leave_u.at[p, k], arrive_u.at[p, k], wd_s.at[p, k], wd_r.at[p, k], ahead)

    def late(k):
        mine = late_r.at[core, k]
        return remote(mine, mine, rd_s.at[k], rd_r.at[k], partner)

    def send_group(g):
        @pl.when(wide_out)
        def _():
            value = leave[pl.ds(g * group, group)].reshape(leave_u.shape[2], modes)
            for p in range(parts):
                leave_u[p, g] = times_table(value, T[1, p * depth:(p + 1) * depth], 1)
                wide_hop(g, p).start()

        for j in range(group):
            send(g * group + j)

    def send(k):
        @pl.when(narrow_out)
        def _():
            hop(k).start()

        late_r[core, k] = leave[k].astype(BF16)
        late(k).start()

    @pl.when(jnp.logical_not(has_prev))
    def _():
        columns = exc[...].T
        for k in range(2):
            @pl.when(core == k)
            def _():
                start = columns[k * count:(k + 1) * count] * damp0
                early_a[...] = start.reshape(early_a.shape)

        start = early_a[...].reshape(count, modes)
        value = times_table(times_table(start, T[0], 1), T[1], 0) * damp1
        leave[...] = value.reshape(leave.shape)

        @pl.loop(0, wides)
        def _(k):
            send_group(k)

    @pl.when(wide_in)
    def _():
        @pl.loop(0, wides)
        def _(k):
            value = jnp.zeros((leave_u.shape[2], modes), F32)
            for p in range(parts):
                wide_hop(k, p).wait_recv()
                value += times_table(arrive_u[p, k], T[0, p * depth:(p + 1) * depth], 0)
            value = value * damp0
            several = pl.ds(k * group, group)
            shape = (group,) + leave.shape[1:]
            leave[several] = times(value, m1.at[0], m1.at[1]).reshape(shape)
            send_group(k)
            early_a[several] = value.reshape(shape)

    @pl.when(narrow_in)
    def _():
        acc[...] = jnp.zeros_like(acc)

        @pl.loop(0, pieces)
        def _(i):
            copy, rows = piece(i)
            copy.wait_recv()
            acc[...] += contract(E[rows], T[0, rows], 0, 0)

        scaled = acc[...] * damp0
        m0[0, own_rows], m0[1, own_rows] = split(scaled)
        product = times(scaled, m1.at[0], m1.at[1])
        pr[0, own_rows], pr[1, own_rows] = split(product)
        mats = [
            remote(ref.at[k, own_rows], ref.at[k, own_rows], mat_s.at[2 * i + k], mat_r.at[2 * i + k], partner)
            for i, ref in enumerate((pr, m0)) for k in range(2)
        ]
        for c in mats:
            c.start()
        for c in mats[:2]:
            c.wait()

        @pl.loop(0, chunks)
        def _(k):
            hop(k).wait_recv()
            leave[k] = times(arrive[k], pr.at[0], pr.at[1])
            send(k)

        for c in mats[2:]:
            c.wait()
        value = times(arrive[...].reshape(count, modes), m0.at[0], m0.at[1])
        early_a[...] = value.reshape(early_a.shape)

    mine = pl.ds(pl.multiple_of(core * count, 16), count)
    rounded[mine] = early_a[...].reshape(count, modes).astype(BF16)
    early = remote(rounded.at[mine], rounded.at[mine], rd_s.at[chunks], rd_r.at[chunks], partner)
    early.start()
    rows = heights // 2
    first = pl.multiple_of(core * rows, 128)

    @pl.loop(0, chunks)
    def _(k):
        late(k).wait()

    out[1] = contract(T[1, pl.ds(first, rows)], late_r[...].reshape(rounded.shape), 1, 1)
    early.wait()
    out[0] = contract(T[0, pl.ds(first, rows)], rounded[...], 1, 1)

    @pl.when(narrow_out)
    def _():
        @pl.loop(0, pieces)
        def _(i):
            piece(i)[0].wait_send()

        @pl.loop(0, chunks)
        def _(k):
            hop(k).wait_send()

    @pl.when(wide_out)
    def _():
        @pl.loop(0, wides)
        def _(k):
            for p in range(parts):
                wide_hop(k, p).wait_send()


def solution(mesh):
    n, cores = mesh.shape["range"], mesh.shape["chip"]

    def on_device(tab, att, exc):
        segs, heights, half = tab.shape
        modes, sources = exc.shape
        wide, pieces, chunks, wides, parts = min(4, n - 1), 8, 8, 4, 4
        rows = sources // cores // chunks
        dma = pltpu.SemaphoreType.DMA
        vmem = pl.BlockSpec(memory_space=pltpu.VMEM)
        return pl.pallas_call(
            functools.partial(kernel, n, wide, pieces, chunks),
            out_shape=pltpu.VMEM((segs, heights // cores, sources), F32),
            in_specs=[pl.BlockSpec(memory_space=pl.ANY), vmem, vmem],
            out_specs=vmem,
            scratch_shapes=[
                pltpu.VMEM((segs, heights, modes), BF16),
                pltpu.VMEM((heights, half), BF16),
                pltpu.VMEM((half, modes), F32),
                pltpu.VMEM((2, modes, modes), BF16),
                pltpu.VMEM((2, modes, modes), BF16),
                pltpu.VMEM((2, modes, modes), BF16),
                pltpu.VMEM((chunks, rows, modes), F32),
                pltpu.VMEM((chunks, rows, modes), F32),
                pltpu.VMEM((parts, wides, rows * chunks // wides, heights // parts), F32),
                pltpu.VMEM((parts, wides, rows * chunks // wides, heights // parts), F32),
                pltpu.VMEM((chunks, rows, modes), F32),
                pltpu.VMEM((cores, chunks, rows, modes), BF16),
                pltpu.VMEM((sources, modes), BF16),
                dma((segs,)),
                dma((segs,)), dma((segs,)),
                dma((pieces,)), dma((pieces,)),
                dma((4,)), dma((4,)),
                dma((chunks,)), dma((chunks,)),
                dma((parts, wides)), dma((parts, wides)),
                dma((chunks + 1,)), dma((chunks + 1,)),
            ],
            compiler_params=pltpu.CompilerParams(
                collective_id=0, has_side_effects=True, vmem_limit_bytes=60 * 2**20
            ),
        )(tab, att, exc)

    return jax.shard_map(
        on_device, mesh=mesh,
        in_specs=(P("range", None, "chip"), P("range", None), P()),
        out_specs=P("range", "chip", None), check_vma=False,
    )
```

```python
import functools

import jax
import jax.numpy as jnp
from jax import lax
from jax.experimental import pallas as pl
from jax.experimental.pallas import tpu as pltpu
from jax.sharding import PartitionSpec as P

MESH = pl.DeviceIdType.MESH
BF16, F32 = jnp.bfloat16, jnp.float32


def contract(a, b, da, db):
    return lax.dot_general(a, b, (((da,), (db,)), ((), ())), preferred_element_type=F32)


def split(x):
    hi = x.astype(BF16)
    return hi, (x - hi.astype(F32)).astype(BF16)


def stacked(x):
    hi = x.astype(BF16).astype(F32)
    return jnp.concatenate([hi, x - hi], axis=0).astype(BF16)


def times(x, w_hi, w_lo):
    rows = x.shape[0]
    both = contract(stacked(x), w_hi[...], 1, 0)
    return both[:rows] + (both[rows:] + contract(x.astype(BF16), w_lo[...], 1, 0))


def times_table(x, table, dim):
    rows = x.shape[0]
    both = contract(stacked(x), table, 1, dim)
    return both[:rows] + both[rows:]


def kernel(
    n, wide, pieces, chunks,
    tab, att, exc, out,
    T, E, acc, m1, m0, pr, arrive, leave, arrive_u, leave_u, early_a, late_r, rounded,
    load_sem, gat_s, gat_r, ear_s, ear_r, mat_s, mat_r, ch_s, ch_r, wd_s, wd_r, rd_s, rd_r,
):
    pos, core = lax.axis_index("range"), lax.axis_index("chip")
    other = 1 - core
    segs, heights, half = tab.shape
    modes = 2 * half
    own_cols = pl.ds(pl.multiple_of(core * half, 128), half)
    own_rows = pl.ds(pl.multiple_of(core * half, 128), half)
    partner, ahead, behind = (pos, other), (pos + 1, core), (pos - 1, core)
    has_next, has_prev = pos < n - 1, pos > 0
    wide_out, narrow_out = pos < wide, jnp.logical_and(pos >= wide, has_next)
    wide_in, narrow_in = jnp.logical_and(has_prev, pos <= wide), pos > wide

    loads = [
        pltpu.make_async_copy(tab.at[s], T.at[s, :, own_cols], load_sem.at[s]) for s in range(segs)
    ]
    for c in loads:
        c.start()
    barrier = pltpu.get_barrier_semaphore()
    pl.semaphore_signal(barrier, inc=1, device_id=partner, device_id_type=MESH)

    @pl.when(has_next)
    def _():
        pl.semaphore_signal(barrier, inc=1, device_id=ahead, device_id_type=MESH)

    @pl.when(has_prev)
    def _():
        pl.semaphore_signal(barrier, inc=1, device_id=behind, device_id_type=MESH)

    pl.semaphore_wait(barrier, 1 + has_next.astype(jnp.int32) + has_prev.astype(jnp.int32))

    def remote(src, dst, s, r, to):
        return pltpu.make_async_remote_copy(
            src_ref=src, dst_ref=dst, send_sem=s, recv_sem=r, device_id=to, device_id_type=MESH
        )

    gathers = [
        remote(tab.at[s], T.at[s, :, own_cols], gat_s.at[s], gat_r.at[s], partner)
        for s in range(segs)
    ]
    for c in gathers:
        c.start()
    size = heights // pieces

    def piece(i):
        rows = pl.ds(pl.multiple_of(i * size, 128), size)
        return remote(tab.at[segs - 1, rows], E.at[rows], ear_s.at[i], ear_r.at[i], ahead), rows

    @pl.when(narrow_out)
    def _():
        @pl.loop(0, pieces)
        def _(i):
            piece(i)[0].start()

    damp0, damp1 = jnp.exp(-att[0:1, :]), jnp.exp(-att[1:2, :])
    for c in loads:
        c.wait()
    for c in gathers:
        c.wait()

    @pl.when(has_prev)
    def _():
        @pl.loop(0, 2)
        def _(j):
            rows = pl.ds(pl.multiple_of(j * half, 128), half)
            m1[0, rows], m1[1, rows] = split(contract(T[0, :, rows], T[1], 0, 0) * damp1)

    count = chunks * arrive.shape[1]

    def hop(k):
        return remote(leave.at[k], arrive.at[k], ch_s.at[k], ch_r.at[k], ahead)

    parts = leave_u.shape[0]
    depth = heights // parts
    wides = leave_u.shape[1]
    group = chunks // wides

    def wide_hop(k, p):
        return remote(leave_u.at[p, k], arrive_u.at[p, k], wd_s.at[p, k], wd_r.at[p, k], ahead)

    def late(k):
        mine = late_r.at[core, k]
        return remote(mine, mine, rd_s.at[k], rd_r.at[k], partner)

    def send_group(g):
        @pl.when(wide_out)
        def _():
            value = leave[pl.ds(g * group, group)].reshape(leave_u.shape[2], modes)
            for p in range(parts):
                leave_u[p, g] = times_table(value, T[1, p * depth:(p + 1) * depth], 1)
                wide_hop(g, p).start()

        for j in range(group):
            send(g * group + j)

    def send(k):
        @pl.when(narrow_out)
        def _():
            hop(k).start()

        late_r[core, k] = leave[k].astype(BF16)
        late(k).start()

    @pl.when(jnp.logical_not(has_prev))
    def _():
        columns = exc[...].T
        for k in range(2):
            @pl.when(core == k)
            def _():
                start = columns[k * count:(k + 1) * count] * damp0
                early_a[...] = start.reshape(early_a.shape)

        start = early_a[...].reshape(count, modes)
        value = times_table(times_table(start, T[0], 1), T[1], 0) * damp1
        leave[...] = value.reshape(leave.shape)

        @pl.loop(0, wides)
        def _(k):
            send_group(k)

    @pl.when(wide_in)
    def _():
        @pl.loop(0, wides)
        def _(k):
            value = jnp.zeros((leave_u.shape[2], modes), F32)
            for p in range(parts):
                wide_hop(k, p).wait_recv()
                value += times_table(arrive_u[p, k], T[0, p * depth:(p + 1) * depth], 0)
            value = value * damp0
            several = pl.ds(k * group, group)
            shape = (group,) + leave.shape[1:]
            leave[several] = times(value, m1.at[0], m1.at[1]).reshape(shape)
            send_group(k)
            early_a[several] = value.reshape(shape)

    @pl.when(narrow_in)
    def _():
        acc[...] = jnp.zeros_like(acc)

        @pl.loop(0, pieces)
        def _(i):
            copy, rows = piece(i)
            copy.wait_recv()
            acc[...] += contract(E[rows], T[0, rows], 0, 0)

        tile = 128
        tiles = half // tile

        def exchange(ref, rows, i):
            return remote(ref.at[:, rows], ref.at[:, rows], mat_s.at[i], mat_r.at[i], partner)

        mats = []
        for t in range(tiles):
            rows = pl.ds(pl.multiple_of(core * half + t * tile, 128), tile)
            scaled = acc[t * tile:(t + 1) * tile] * damp0
            m0[0, rows], m0[1, rows] = split(scaled)
            pr[0, rows], pr[1, rows] = split(times(scaled, m1.at[0], m1.at[1]))
            mats.append(exchange(pr, rows, t))
            mats[t].start()
        mats.append(exchange(m0, own_rows, tiles))
        mats[tiles].start()
        for c in mats[:tiles]:
            c.wait()

        @pl.loop(0, chunks)
        def _(k):
            hop(k).wait_recv()
            leave[k] = times(arrive[k], pr.at[0], pr.at[1])
            send(k)

        mats[tiles].wait()
        value = times(arrive[...].reshape(count, modes), m0.at[0], m0.at[1])
        early_a[...] = value.reshape(early_a.shape)

    mine = pl.ds(pl.multiple_of(core * count, 16), count)
    rounded[mine] = early_a[...].reshape(count, modes).astype(BF16)
    early = remote(rounded.at[mine], rounded.at[mine], rd_s.at[chunks], rd_r.at[chunks], partner)
    early.start()
    rows = heights // 2
    first = pl.multiple_of(core * rows, 128)

    @pl.loop(0, chunks)
    def _(k):
        late(k).wait()

    out[1] = contract(T[1, pl.ds(first, rows)], late_r[...].reshape(rounded.shape), 1, 1)
    early.wait()
    out[0] = contract(T[0, pl.ds(first, rows)], rounded[...], 1, 1)

    @pl.when(narrow_out)
    def _():
        @pl.loop(0, pieces)
        def _(i):
            piece(i)[0].wait_send()

        @pl.loop(0, chunks)
        def _(k):
            hop(k).wait_send()

    @pl.when(wide_out)
    def _():
        @pl.loop(0, wides)
        def _(k):
            for p in range(parts):
                wide_hop(k, p).wait_send()


def solution(mesh):
    n, cores = mesh.shape["range"], mesh.shape["chip"]

    def on_device(tab, att, exc):
        segs, heights, half = tab.shape
        modes, sources = exc.shape
        wide, pieces, chunks, wides, parts = min(4, n - 1), 8, 8, 4, 4
        rows = sources // cores // chunks
        dma = pltpu.SemaphoreType.DMA
        vmem = pl.BlockSpec(memory_space=pltpu.VMEM)
        return pl.pallas_call(
            functools.partial(kernel, n, wide, pieces, chunks),
            out_shape=pltpu.VMEM((segs, heights // cores, sources), F32),
            in_specs=[pl.BlockSpec(memory_space=pl.ANY), vmem, vmem],
            out_specs=vmem,
            scratch_shapes=[
                pltpu.VMEM((segs, heights, modes), BF16),
                pltpu.VMEM((heights, half), BF16),
                pltpu.VMEM((half, modes), F32),
                pltpu.VMEM((2, modes, modes), BF16),
                pltpu.VMEM((2, modes, modes), BF16),
                pltpu.VMEM((2, modes, modes), BF16),
                pltpu.VMEM((chunks, rows, modes), F32),
                pltpu.VMEM((chunks, rows, modes), F32),
                pltpu.VMEM((parts, wides, rows * chunks // wides, heights // parts), F32),
                pltpu.VMEM((parts, wides, rows * chunks // wides, heights // parts), F32),
                pltpu.VMEM((chunks, rows, modes), F32),
                pltpu.VMEM((cores, chunks, rows, modes), BF16),
                pltpu.VMEM((sources, modes), BF16),
                dma((segs,)),
                dma((segs,)), dma((segs,)),
                dma((pieces,)), dma((pieces,)),
                dma((half // 128 + 1,)), dma((half // 128 + 1,)),
                dma((chunks,)), dma((chunks,)),
                dma((parts, wides)), dma((parts, wides)),
                dma((chunks + 1,)), dma((chunks + 1,)),
            ],
            compiler_params=pltpu.CompilerParams(
                collective_id=0, has_side_effects=True, vmem_limit_bytes=60 * 2**20
            ),
        )(tab, att, exc)

    return jax.shard_map(
        on_device, mesh=mesh,
        in_specs=(P("range", None, "chip"), P("range", None), P()),
        out_specs=P("range", "chip", None), check_vma=False,
    )
```

```python
import functools

import jax
import jax.numpy as jnp
from jax import lax
from jax.experimental import pallas as pl
from jax.experimental.pallas import tpu as pltpu
from jax.sharding import PartitionSpec as P

MESH = pl.DeviceIdType.MESH
BF16, F32 = jnp.bfloat16, jnp.float32


def contract(a, b, da, db):
    return lax.dot_general(a, b, (((da,), (db,)), ((), ())), preferred_element_type=F32)


def split(x):
    hi = x.astype(BF16)
    return hi, (x - hi.astype(F32)).astype(BF16)


def stacked(x):
    hi = x.astype(BF16).astype(F32)
    return jnp.concatenate([hi, x - hi], axis=0).astype(BF16)


def times(x, w_hi, w_lo):
    rows = x.shape[0]
    both = contract(stacked(x), w_hi[...], 1, 0)
    return both[:rows] + (both[rows:] + contract(x.astype(BF16), w_lo[...], 1, 0))


def times_table(x, table, dim):
    rows = x.shape[0]
    both = contract(stacked(x), table, 1, dim)
    return both[:rows] + both[rows:]


def kernel(
    n, wide, pieces, chunks,
    tab, att, exc, out,
    T, E, acc, m1, m0, pr, arrive, leave, arrive_u, leave_u, early_a, late_r, rounded,
    load_sem, gat_s, gat_r, ear_s, ear_r, mat_s, mat_r, ch_s, ch_r, wd_s, wd_r, rd_s, rd_r,
):
    pos, core = lax.axis_index("range"), lax.axis_index("chip")
    other = 1 - core
    segs, heights, half = tab.shape
    modes = 2 * half
    own_cols = pl.ds(pl.multiple_of(core * half, 128), half)
    own_rows = pl.ds(pl.multiple_of(core * half, 128), half)
    partner, ahead, behind = (pos, other), (pos + 1, core), (pos - 1, core)
    has_next, has_prev = pos < n - 1, pos > 0
    wide_out, narrow_out = pos < wide, jnp.logical_and(pos >= wide, has_next)
    wide_in, narrow_in = jnp.logical_and(has_prev, pos <= wide), pos > wide

    loads = [
        pltpu.make_async_copy(tab.at[s], T.at[s, :, own_cols], load_sem.at[s]) for s in range(segs)
    ]
    for c in loads:
        c.start()
    barrier = pltpu.get_barrier_semaphore()
    pl.semaphore_signal(barrier, inc=1, device_id=partner, device_id_type=MESH)

    @pl.when(has_next)
    def _():
        pl.semaphore_signal(barrier, inc=1, device_id=ahead, device_id_type=MESH)

    @pl.when(has_prev)
    def _():
        pl.semaphore_signal(barrier, inc=1, device_id=behind, device_id_type=MESH)

    pl.semaphore_wait(barrier, 1 + has_next.astype(jnp.int32) + has_prev.astype(jnp.int32))

    def remote(src, dst, s, r, to):
        return pltpu.make_async_remote_copy(
            src_ref=src, dst_ref=dst, send_sem=s, recv_sem=r, device_id=to, device_id_type=MESH
        )

    gathers = [
        remote(tab.at[s], T.at[s, :, own_cols], gat_s.at[s], gat_r.at[s], partner)
        for s in range(segs)
    ]
    for c in gathers:
        c.start()
    size = heights // pieces

    def piece(i):
        rows = pl.ds(pl.multiple_of(i * size, 128), size)
        return remote(tab.at[segs - 1, rows], E.at[rows], ear_s.at[i], ear_r.at[i], ahead), rows

    @pl.when(narrow_out)
    def _():
        @pl.loop(0, pieces)
        def _(i):
            piece(i)[0].start()

    damp0, damp1 = jnp.exp(-att[0:1, :]), jnp.exp(-att[1:2, :])
    for c in loads:
        c.wait()
    for c in gathers:
        c.wait()

    @pl.when(has_prev)
    def _():
        @pl.loop(0, 2)
        def _(j):
            rows = pl.ds(pl.multiple_of(j * half, 128), half)
            m1[0, rows], m1[1, rows] = split(contract(T[0, :, rows], T[1], 0, 0) * damp1)

    count = chunks * arrive.shape[1]

    def hop(k):
        return remote(leave.at[k], arrive.at[k], ch_s.at[k], ch_r.at[k], ahead)

    parts = leave_u.shape[0]
    depth = heights // parts
    wides = leave_u.shape[1]
    group = chunks // wides

    def wide_hop(k, p):
        return remote(leave_u.at[p, k], arrive_u.at[p, k], wd_s.at[p, k], wd_r.at[p, k], ahead)

    def late(k):
        mine = late_r.at[core, k]
        return remote(mine, mine, rd_s.at[k], rd_r.at[k], partner)

    def send_group(g):
        @pl.when(wide_out)
        def _():
            value = leave[pl.ds(g * group, group)].reshape(leave_u.shape[2], modes)
            for p in range(parts):
                leave_u[p, g] = times_table(value, T[1, p * depth:(p + 1) * depth], 1)
                wide_hop(g, p).start()

        for j in range(group):
            send(g * group + j)

    def send(k):
        @pl.when(narrow_out)
        def _():
            hop(k).start()

        late_r[core, k] = leave[k].astype(BF16)
        late(k).start()

    @pl.when(jnp.logical_not(has_prev))
    def _():
        columns = exc[...].T
        for k in range(2):
            @pl.when(core == k)
            def _():
                start = columns[k * count:(k + 1) * count] * damp0
                early_a[...] = start.reshape(early_a.shape)

        start = early_a[...].reshape(count, modes)
        value = times_table(times_table(start, T[0], 1), T[1], 0) * damp1
        leave[...] = value.reshape(leave.shape)

        @pl.loop(0, wides)
        def _(k):
            send_group(k)

    @pl.when(wide_in)
    def _():
        @pl.loop(0, wides)
        def _(k):
            value = jnp.zeros((leave_u.shape[2], modes), F32)
            for p in range(parts):
                wide_hop(k, p).wait_recv()
                value += times_table(arrive_u[p, k], T[0, p * depth:(p + 1) * depth], 0)
            value = value * damp0
            several = pl.ds(k * group, group)
            shape = (group,) + leave.shape[1:]
            leave[several] = times(value, m1.at[0], m1.at[1]).reshape(shape)
            send_group(k)
            early_a[several] = value.reshape(shape)

    @pl.when(narrow_in)
    def _():
        acc[...] = jnp.zeros_like(acc)

        @pl.loop(0, pieces)
        def _(i):
            copy, rows = piece(i)
            copy.wait_recv()
            acc[...] += contract(E[rows], T[0, rows], 0, 0)

        tile = 128
        tiles = half // tile

        def exchange(ref, rows, i):
            return remote(ref.at[:, rows], ref.at[:, rows], mat_s.at[i], mat_r.at[i], partner)

        mats = []
        for t in range(tiles):
            rows = pl.ds(pl.multiple_of(core * half + t * tile, 128), tile)
            scaled = acc[t * tile:(t + 1) * tile] * damp0
            m0[0, rows], m0[1, rows] = split(scaled)
            pr[0, rows], pr[1, rows] = split(times(scaled, m1.at[0], m1.at[1]))
            mats.append(exchange(pr, rows, t))
            mats[t].start()
        mats.append(exchange(m0, own_rows, tiles))
        mats[tiles].start()
        for c in mats[:tiles]:
            c.wait()

        @pl.loop(0, chunks)
        def _(k):
            hop(k).wait_recv()
            leave[k] = times(arrive[k], pr.at[0], pr.at[1])
            send(k)

        mats[tiles].wait()
        value = times(arrive[...].reshape(count, modes), m0.at[0], m0.at[1])
        early_a[...] = value.reshape(early_a.shape)

    mine = pl.ds(pl.multiple_of(core * count, 16), count)
    rounded[mine] = early_a[...].reshape(count, modes).astype(BF16)
    early = remote(rounded.at[mine], rounded.at[mine], rd_s.at[chunks], rd_r.at[chunks], partner)
    early.start()
    rows = heights // 2
    first = pl.multiple_of(core * rows, 128)

    @pl.loop(0, chunks)
    def _(k):
        late(k).wait()

    out[1] = contract(T[1, pl.ds(first, rows)], late_r[...].reshape(rounded.shape), 1, 1)
    early.wait()
    out[0] = contract(T[0, pl.ds(first, rows)], rounded[...], 1, 1)

    @pl.when(narrow_out)
    def _():
        @pl.loop(0, pieces)
        def _(i):
            piece(i)[0].wait_send()

        @pl.loop(0, chunks)
        def _(k):
            hop(k).wait_send()

    @pl.when(wide_out)
    def _():
        @pl.loop(0, wides)
        def _(k):
            for p in range(parts):
                wide_hop(k, p).wait_send()


def solution(mesh):
    n, cores = mesh.shape["range"], mesh.shape["chip"]

    def on_device(tab, att, exc):
        segs, heights, half = tab.shape
        modes, sources = exc.shape
        wide, pieces, chunks, wides, parts = min(5, n - 1), 8, 8, 4, 4
        rows = sources // cores // chunks
        dma = pltpu.SemaphoreType.DMA
        vmem = pl.BlockSpec(memory_space=pltpu.VMEM)
        return pl.pallas_call(
            functools.partial(kernel, n, wide, pieces, chunks),
            out_shape=pltpu.VMEM((segs, heights // cores, sources), F32),
            in_specs=[pl.BlockSpec(memory_space=pl.ANY), vmem, vmem],
            out_specs=vmem,
            scratch_shapes=[
                pltpu.VMEM((segs, heights, modes), BF16),
                pltpu.VMEM((heights, half), BF16),
                pltpu.VMEM((half, modes), F32),
                pltpu.VMEM((2, modes, modes), BF16),
                pltpu.VMEM((2, modes, modes), BF16),
                pltpu.VMEM((2, modes, modes), BF16),
                pltpu.VMEM((chunks, rows, modes), F32),
                pltpu.VMEM((chunks, rows, modes), F32),
                pltpu.VMEM((parts, wides, rows * chunks // wides, heights // parts), F32),
                pltpu.VMEM((parts, wides, rows * chunks // wides, heights // parts), F32),
                pltpu.VMEM((chunks, rows, modes), F32),
                pltpu.VMEM((cores, chunks, rows, modes), BF16),
                pltpu.VMEM((sources, modes), BF16),
                dma((segs,)),
                dma((segs,)), dma((segs,)),
                dma((pieces,)), dma((pieces,)),
                dma((half // 128 + 1,)), dma((half // 128 + 1,)),
                dma((chunks,)), dma((chunks,)),
                dma((parts, wides)), dma((parts, wides)),
                dma((chunks + 1,)), dma((chunks + 1,)),
            ],
            compiler_params=pltpu.CompilerParams(
                collective_id=0, has_side_effects=True, vmem_limit_bytes=60 * 2**20
            ),
        )(tab, att, exc)

    return jax.shard_map(
        on_device, mesh=mesh,
        in_specs=(P("range", None, "chip"), P("range", None), P()),
        out_specs=P("range", "chip", None), check_vma=False,
    )
```
